32 devices in a mesh: row: 8 (over z, x), col: 4 (over y, core).
Axes of the slice: x: 2, y: 2, z: 4, core: 2. Of those that a mesh axis runs over, the one named last changes fastest.
Arguments:
- near_blocks: bfloat16 [4096, 4096], P('row', 'col'), may hold values from -0.1875 to 0.1875
- pattern: int32 [8, 4], P('row', 'col'), may hold values 0 or 1
- iterate: bfloat16 [4096, 256], P('col'), may hold values from -6 to 6
- right_side: float32 [4096, 256], P(('row', 'col')), may hold values from -6 to 6
- basis: bfloat16 [4096, 512], P(('row', 'col')), may hold values from -0.1875 to 0.1875
- leaf_weight: float32 [4096], P(('row', 'col')), may hold values from 0.25 to 4
- transfers: bfloat16 [6, 512, 512], P(None, 'col'), may hold values from -0.1875 to 0.1875
- inverses: bfloat16 [7, 512, 512], P(None, 'col'), may hold values from -0.25 to 0.25
Outputs:
- correction: float32 [4096, 256], P(('row', 'col'))
The draws below stay inside these ranges and needn't reach their ends.
Inputs may be any that keep to these rules, and one draw needn't show every extreme that they name: `pattern`: 0 or 1 for each pair of a row shard and a leaf column.
All inputs are finite; a program needn't handle non-finite values.
Results may differ from the reference program's by a relative error of at most 0.0003.
Values may be sent and summed in bfloat16 or wider, within the bound.
A program may use at most 64 MiB of HBM per device.

```python
import math
import jax
import jax.numpy as jnp
from jax import lax

LEAF = 1024
RANK = 512
RHS = 256
ROWS_DEV = 512
ORDER = 4096
N_ROW = 8
N_COL = 4


def place_ends(entries, own_key, least, top_value):
    place = [jax.random.randint(jax.random.fold_in(own_key, axis), (), 0, length) for axis, length in enumerate(entries.shape)]
    main_axis = entries.shape.index(max(entries.shape))
    next_to = place[:main_axis] + [(place[main_axis] + 1) % entries.shape[main_axis]] + place[main_axis + 1:]
    return entries.at[tuple(place)].set(least).at[tuple(next_to)].set(top_value)


def strengthened(drawn, own_key, source, target, shards_of, factor):
    owner, partner = [(jnp.arange(drawn.shape[dim]) // (drawn.shape[dim] // shards_of)).reshape([-1 if axis == dim else 1 for axis in range(drawn.ndim)]) for dim in (source, target)]
    chosen = jax.random.permutation(own_key, shards_of)[partner]
    strong = (owner == chosen) | (owner == (partner + shards_of // 2) % shards_of)
    return jnp.where(strong, factor * drawn, drawn)


def shard_levels(stream_key, shape, shards, smallest, high):
    factor_of, own = 1.0, jax.random.fold_in(stream_key, 6)
    for axis_at, blocks in shards:
        steps = jnp.exp(jax.random.uniform(jax.random.fold_in(own, axis_at), (blocks,), jnp.float32, smallest / len(shards), high / len(shards)))
        factor_of = factor_of * jnp.repeat(steps, shape[axis_at] // blocks).reshape([-1 if axis == axis_at else 1 for axis in range(len(shape))])
    return factor_of


def bell_draw(rng, dims, spread, bound, cuts=(), kind=jnp.bfloat16):
    values = jax.random.normal(rng, dims, jnp.float32) * spread
    if len(cuts) > 0:
        values = shard_levels(rng, dims, cuts, -0.22, 0.18) * values
    return jnp.clip(values, min=-bound, max=bound).astype(kind)


def bell_draw_with(own_key, extent, spread, bound, pieces, heavy, held_as=jnp.bfloat16):
    entries = spread * jax.random.normal(own_key, extent, jnp.float32)
    if pieces:
        entries = entries * shard_levels(own_key, extent, pieces, -0.22, 0.18)
    return jnp.clip(strengthened(entries, jax.random.fold_in(own_key, 3), *heavy), -bound, bound).astype(held_as)


def setup_inputs(seed: int = 0) -> dict:
    seeds = jax.random.split(jax.random.key(seed), 9)
    near_blocks = bell_draw_with(seeds[0], (ORDER, ORDER), (LEAF * N_COL // 2) ** -0.5, 0.1875, ((0, 8), (1, 4)), (1, 0, 8, 2.0))
    pattern = place_ends((jax.random.randint(seeds[1], (N_ROW, N_COL), 0, 2) < 1).astype(jnp.int32), jax.random.fold_in(seeds[1], 1), 0, 1)
    iterate = bell_draw(seeds[2], (ORDER, RHS), 1.0, 6.0, ((0, 4),))
    right_side = bell_draw(seeds[3], (ORDER, RHS), 1.0, 6.0, ((0, 32),), jnp.float32)
    basis = bell_draw(seeds[4], (ORDER, RANK), LEAF ** -0.5, 0.1875, ((0, 32),))
    leaf_weight = jnp.clip(jnp.exp(math.log(4.0) - 2.7725887 * jax.random.uniform(seeds[5], (ORDER,), jnp.float32) ** shard_levels(seeds[5], (ORDER,), ((0, 32),), -0.2, 0.2)), 0.25, 4.0)
    transfers = bell_draw(seeds[6], (2 * N_COL - 2, RANK, RANK), (2 * RANK) ** -0.5, 0.1875, ((1, 4),))
    inverses = bell_draw(seeds[7], (2 * N_COL - 1, RANK, RANK), RANK ** -0.5, 0.25, ((1, 4),))
    return dict(near_blocks=near_blocks, pattern=pattern, iterate=iterate, right_side=right_side, basis=basis, leaf_weight=leaf_weight, transfers=transfers, inverses=inverses)


exact_mode = lax.Precision.HIGHEST


def matmul(lhs_matrix, rhs_matrix):
    return jnp.matmul(lhs_matrix, rhs_matrix, precision=exact_mode)


def reference(near_blocks, pattern, iterate, right_side, basis, leaf_weight, transfers, inverses):
    order_total = LEAF * N_COL
    applied = jnp.zeros((order_total, RHS), jnp.float32)
    for column in range(N_COL):
        near_slab = near_blocks[:, column * LEAF:(column + 1) * LEAF]
        near_term = jnp.dot(near_slab, iterate[column * LEAF:(column + 1) * LEAF], preferred_element_type=jnp.float32)
        present = jnp.repeat(pattern[:, column].astype(jnp.float32), ROWS_DEV)
        applied = applied + present[:, None] * near_term
    residual = right_side - applied
    basis_wide = basis.astype(jnp.float32).reshape(N_COL, LEAF, RANK)
    weighted = leaf_weight.reshape(N_COL, LEAF, 1) * basis_wide
    basis_turned = jnp.swapaxes(basis_wide, 1, 2)
    schur_block = matmul(basis_turned, weighted)
    projected = matmul(basis_turned, residual.reshape(N_COL, LEAF, RHS))
    levels = N_COL.bit_length() - 1
    kept_levels = []
    node_count = N_COL
    level_start = 0
    for tree_level in range(levels):
        edge_stack = transfers[level_start:level_start + node_count].astype(jnp.float32)
        product = matmul(schur_block, edge_stack)
        kept_levels.append((product, projected))
        edge_turned = jnp.swapaxes(edge_stack, 1, 2)
        lifted_schur = matmul(edge_turned, product)
        lifted_proj = matmul(edge_turned, projected)
        schur_block = lifted_schur[0::2] + lifted_schur[1::2]
        projected = lifted_proj[0::2] + lifted_proj[1::2]
        level_start = level_start + node_count
        node_count = node_count // 2
    root_inverse = inverses[2 * N_COL - 2:2 * N_COL - 1].astype(jnp.float32)
    node_correction = matmul(root_inverse, projected)
    for tree_level in range(levels - 1, -1, -1):
        product, projected = kept_levels[tree_level]
        node_count = N_COL >> tree_level
        level_start = 2 * N_COL - ((2 * N_COL) >> tree_level)
        parent = jnp.repeat(node_correction, 2, axis=0)
        adjusted = projected - matmul(product, parent)
        node_inverse = inverses[level_start:level_start + node_count].astype(jnp.float32)
        node_correction = matmul(node_inverse, adjusted)
    return matmul(basis_wide, node_correction).reshape(order_total, RHS)
```

```python
import functools

import jax
import jax.numpy as jnp
from jax import lax
from jax.experimental import pallas as pl
from jax.experimental.pallas import tpu as pltpu
from jax.sharding import PartitionSpec as P

F32, BF16 = jnp.float32, jnp.bfloat16


def thin(x, mat, turned):
    n = x.shape[0]
    high = x.astype(BF16).astype(F32)
    both = jnp.concatenate([high, x - high], axis=0).astype(BF16)
    dims = (((1,), (1 if turned else 0,)), ((), ()))
    r = lax.dot_general(both, mat, dims, preferred_element_type=F32)
    return r[:n] + r[n:]


def split(ref, x):
    high = x.astype(BF16)
    ref[0] = high
    ref[1] = (x - high.astype(F32)).astype(BF16)


def pair_dot(lhs, rhs, dims):
    total = None
    for a in lhs:
        for b in rhs:
            r = lax.dot_general(a, b, (dims, ((), ())), preferred_element_type=F32)
            total = r if total is None else total + r
    return total


def counts(cols, levels):
    chips = cols
    mats = 2 * levels + 1
    swaps = levels + levels * (levels - 1) // 2
    remote = (
        4 * (cols // 2) - 1
        + 2 * cols - 1
        + mats * (2 * (cols // 2 - 1) + 1)
        + 1 + chips - 1
        + swaps
        + 2 * cols - 1
    )
    return chips, mats, swaps, remote


def kernel(
    cols, levels,
    near, pattern, iterate, right, basis, weight, transfers, inverses,
    out,
    near_v, iter_v, right_v, vfull, dfull, mats, part, corebuf, red, halfbuf,
    swap_out, swap_in, fin_out, fin_in, weighted, block, products, local_sem, send_sem, recv_sem,
):
    chips, n_mats, _, _ = counts(cols, levels)
    row, col = lax.axis_index("row"), lax.axis_index("col")
    leaf, half = row // 2, row % 2
    lane, core = col // 2, col % 2
    lanes = cols // 2
    chip = half * lanes + lane
    group = 2 * cols
    rhs = iterate.shape[1]
    n = rhs // group
    own_rows = basis.shape[0]
    mat_rows = transfers.shape[1]
    partner = (row, col + 1 - 2 * core)

    def chip_device(c, k):
        return (leaf * 2 + c // lanes, (c % lanes) * 2 + k)

    def place(c, k):
        return (c // lanes) * cols + (c % lanes) * 2 + k

    def rows_at(c, k, size):
        return pl.ds(pl.multiple_of(place(c, k) * size, size), size)

    def sibling(bit):
        b = (leaf // 2**bit) % 2
        return ((leaf + (1 - 2 * b) * 2**bit) * 2 + half, col)

    used = [0]
    started = []

    def send(src, dst, device):
        k = used[0]
        used[0] += 1
        copy = pltpu.make_async_remote_copy(
            src_ref=src, dst_ref=dst, send_sem=send_sem.at[k], recv_sem=recv_sem.at[k],
            device_id=device, device_id_type=pl.DeviceIdType.MESH,
        )
        copy.start()
        started.append(copy)
        return copy

    locals_used = [0]

    def local(src, dst):
        k = locals_used[0]
        locals_used[0] += 1
        copy = pltpu.make_async_copy(src, dst, local_sem.at[k])
        copy.start()
        return copy

    offsets = [(1, d) for d in range(1, lanes)] + [(1, 0)] + [(0, d) for d in range(1, lanes)]

    def ahead(o):
        return ((half + o[0]) % 2) * lanes + (lane + o[1]) % lanes

    def behind(o):
        return ((half + o[0]) % 2) * lanes + (lane + lanes - o[1]) % lanes

    barrier = pltpu.get_barrier_semaphore()
    others = []
    for d in range(chips):
        c = (chip + d) % chips
        if d > 0:
            others.append(chip_device(c, core))
        others.append(chip_device(c, 1 - core))
    others += [sibling(b) for b in range(levels)]
    for device in others:
        pl.semaphore_signal(
            barrier, inc=1, device_id=device, device_id_type=pl.DeviceIdType.MESH
        )
    mine = rows_at(chip, core, own_rows)
    near_copy = local(near, near_v)
    iter_copy = local(iterate, iter_v)
    mine_in_half = pl.ds(pl.multiple_of(col * own_rows, own_rows), own_rows)
    aligned = own_rows % 128 == 0
    if not aligned:
        right_v[...] = jnp.zeros_like(right_v)
    right_copy = local(right, right_v if aligned else right_v.at[mine_in_half])
    base_copy = local(basis, vfull.at[mine])
    weight_copy = local(weight, dfull.at[place(chip, core)])

    def source(m):
        k = m if m < levels else m - levels
        index = 2 * cols - (2 * cols // 2**k) + leaf // 2**k
        return (transfers if m < levels else inverses).at[index]

    order = list(range(levels)) + [levels + k for k in range(levels, -1, -1)]
    own_mat = pl.ds(pl.multiple_of(col * mat_rows, mat_rows), mat_rows)
    mat_local = {m: local(source(m), mats.at[m, own_mat]) for m in order}

    pl.semaphore_wait(barrier, len(others))

    across = ((leaf * 2 + 1 - half), col)
    base_lane = [
        send(basis, vfull.at[mine], (row, ((lane + d) % lanes) * 2 + core))
        for d in range(1, lanes)
    ]
    base_across = send(basis, vfull.at[mine], across)
    base_partner = send(basis, vfull.at[mine], partner)

    def base_slot(h, d):
        return vfull.at[rows_at(h * lanes + (lane + lanes - d) % lanes, core, own_rows)]

    weight_sends = []
    for d in range(chips):
        c = (chip + d) % chips
        for k in ([core, 1 - core] if d > 0 else [1 - core]):
            weight_sends.append(
                send(weight, dfull.at[place(chip, core)], chip_device(c, k))
            )
    mat_far, mat_near, mat_forward = {}, {}, {}

    def start_mat(m):
        mat_far[m] = [
            send(source(m), mats.at[m, own_mat], (row, ((lane + d) % lanes) * 2 + core))
            for d in range(1, lanes)
        ]
        mat_near[m] = send(source(m), mats.at[m, own_mat], partner)

    def forward_mat(m):
        mat_forward[m] = []
        for d in range(1, lanes):
            mat_far[m][d - 1].wait_recv()
            came = ((lane + lanes - d) % lanes) * 2 + core
            slot = mats.at[m, pl.ds(pl.multiple_of(came * mat_rows, mat_rows), mat_rows)]
            mat_forward[m].append(send(slot, slot, partner))

    def finish_mat(m):
        mat_local[m].wait()
        mat_near[m].wait_recv()
        for copy in mat_forward[m]:
            copy.wait_recv()

    start_mat(order[0])

    near_copy.wait()
    iter_copy.wait()
    right_copy.wait()
    present = pattern[0, 0].astype(F32)
    turned = lax.dot_general(
        iter_v[...], near_v[...], (((0,), (1,)), ((), ())), preferred_element_type=F32
    )
    if aligned:
        part[...] = -present * turned
        part[:, mine_in_half] = part[:, mine_in_half] + right_v[...].T
    else:
        part[...] = right_v[...].T - present * turned

    wide = rhs // 2
    core_send = send(
        part.at[pl.ds(pl.multiple_of((1 - core) * wide, wide), wide)], corebuf, partner
    )
    core_send.wait_recv()
    base_forward = []
    for d in range(1, lanes):
        base_lane[d - 1].wait_recv()
        base_forward.append(send(base_slot(half, d), base_slot(half, d), partner))
    applied = part[pl.ds(pl.multiple_of(core * wide, wide), wide), :] + corebuf[...]
    base_copy.wait()
    base_partner.wait_recv()
    for copy in base_forward:
        copy.wait_recv()
    half_rows = near.shape[0]
    half_base = vfull[pl.ds(pl.multiple_of(half * half_rows, half_rows), half_rows), :]
    red[...] = thin(applied, half_base, False)
    half_sends = []
    for o in offsets:
        c = ahead(o)
        half_sends.append(
            send(
                red.at[pl.ds(pl.multiple_of(c * n, n), n)],
                halfbuf.at[chip],
                chip_device(c, core),
            )
        )
    relays = [send(base_slot(half, d), base_slot(half, d), across) for d in range(1, lanes)]
    for m in order[1:]:
        start_mat(m)
    base_across.wait_recv()
    far_forward = [send(base_slot(1 - half, 0), base_slot(1 - half, 0), partner)]

    def forward_relays():
        for d in range(1, lanes):
            relays[d - 1].wait_recv()
            far_forward.append(send(base_slot(1 - half, d), base_slot(1 - half, d), partner))

    forward_mat(order[0])
    gathered = red[pl.ds(pl.multiple_of(chip * n, n), n), :]
    for o, copy in zip(offsets, half_sends):
        copy.wait_recv()
        gathered = gathered + halfbuf[behind(o)]
    swaps_used = [0]

    def swap_sum(x, bit, meanwhile=(), then=None):
        k = swaps_used[0]
        swaps_used[0] += 1
        swap_out[k] = x
        copy = send(swap_out.at[k], swap_in.at[k], sibling(bit))
        for m in meanwhile:
            forward_mat(m)
        if then is not None:
            then()
        copy.wait_recv()
        return x + swap_in[k]

    def form_leaf():
        weight_copy.wait()
        for copy in far_forward:
            copy.wait_recv()
        for copy in weight_sends:
            copy.wait_recv()
        weights = jnp.concatenate([dfull[p] for p in range(group)], axis=0).T
        for p in range(group):
            rows = pl.ds(p * own_rows, own_rows)
            scaled = weights[:, p:p + 1] * vfull[rows, :].astype(F32)
            high = scaled.astype(BF16)
            weighted[0, rows, :] = high
            weighted[1, rows, :] = (scaled - high.astype(F32)).astype(BF16)
        split(block, pair_dot([vfull[...]], [weighted[0], weighted[1]], ((0,), (0,))))

    def form_products():
        split(products.at[0], pair_dot([block[0], block[1]], [mats[0]], ((1,), (0,))))

    projected = [gathered]
    pending = order[1:]
    for k in range(levels):
        finish_mat(k)
        lifted = thin(projected[k], mats[k], False)
        now, pending = pending[:1], pending[1:]
        if k < levels - 1:
            projected.append(swap_sum(lifted, k, now, forward_relays if k == 0 else None))
        else:
            projected.append(swap_sum(lifted, k, now, form_leaf))
    finish_mat(2 * levels)
    correction = thin(projected[levels], mats[2 * levels], True)
    for k in range(levels - 1, -1, -1):
        if k == 0:
            s = thin(correction, products[0, 0], True) + thin(correction, products[0, 1], True)
        else:
            y = correction
            for j in range(k, -1, -1):
                y = thin(y, mats[j], True)
            s = thin(y, block[0], True) + thin(y, block[1], True)
        for j in range(k):
            s = thin(s, mats[j], False)
            s = swap_sum(s, j, pending[:1], form_products if k == 1 else None)
            pending = pending[1:]
        for m in pending[:1] if levels + k in pending else ():
            forward_mat(m)
            pending = pending[1:]
        finish_mat(levels + k)
        correction = thin(projected[k] - s, mats[levels + k], True)
    rows = thin(correction, vfull[...], True)
    for p in range(group):
        fin_out[p] = rows[:, p * own_rows:(p + 1) * own_rows]
    first = (core * chips + chip) * n
    slot = pl.ds(pl.multiple_of(first, n), n)
    fin_sends = []
    for o in offsets + [(0, 0)]:
        c = ahead(o)
        for k in ([core, 1 - core] if o != (0, 0) else [1 - core]):
            fin_sends.append(send(fin_out.at[place(c, k)], fin_in.at[slot], chip_device(c, k)))
    fin_in[slot, :] = fin_out[place(chip, core)]
    for copy in fin_sends:
        copy.wait_recv()
    out[...] = fin_in[...]
    for copy in started:
        copy.wait_send()


def on_device(near_blocks, pattern, iterate, right_side, basis, leaf_weight, transfers, inverses):
    cols = lax.axis_size("col")
    levels = cols.bit_length() - 1
    chips, n_mats, swaps, remote = counts(cols, levels)
    group = 2 * cols
    rank = basis.shape[1]
    own_rows = basis.shape[0]
    rhs = iterate.shape[1]
    n = rhs // group
    half_rows = near_blocks.shape[0]
    any_spec = pl.BlockSpec(memory_space=pl.ANY)
    turned = pl.pallas_call(
        functools.partial(kernel, cols, levels),
        out_shape=pltpu.VMEM((rhs, own_rows), F32),
        in_specs=[any_spec, pl.BlockSpec(memory_space=pltpu.SMEM)] + [any_spec] * 6,
        out_specs=pl.BlockSpec(memory_space=pltpu.VMEM),
        scratch_shapes=[
            pltpu.VMEM(near_blocks.shape, BF16),
            pltpu.VMEM(iterate.shape, BF16),
            pltpu.VMEM((own_rows if own_rows % 128 == 0 else half_rows, rhs), F32),
            pltpu.VMEM((2 * half_rows, rank), BF16),
            pltpu.VMEM((group, 1, own_rows), F32),
            pltpu.VMEM((n_mats, rank, rank), BF16),
            pltpu.VMEM((rhs, half_rows), F32),
            pltpu.VMEM((rhs // 2, half_rows), F32),
            pltpu.VMEM((rhs // 2, rank), F32),
            pltpu.VMEM((chips, n, rank), F32),
            pltpu.VMEM((swaps, n, rank), F32),
            pltpu.VMEM((swaps, n, rank), F32),
            pltpu.VMEM((group, n, own_rows), F32),
            pltpu.VMEM((rhs, own_rows), F32),
            pltpu.VMEM((2, 2 * half_rows, rank), BF16),
            pltpu.VMEM((2, rank, rank), BF16),
            pltpu.VMEM((levels, 2, rank, rank), BF16),
            pltpu.SemaphoreType.DMA((5 + n_mats,)),
            pltpu.SemaphoreType.DMA((remote,)),
            pltpu.SemaphoreType.DMA((remote,)),
        ],
        compiler_params=pltpu.CompilerParams(collective_id=0, has_side_effects=True),
    )(
        near_blocks, pattern, iterate, right_side, basis,
        leaf_weight.reshape(1, own_rows), transfers, inverses,
    )
    return turned.T


def solution(mesh):
    placed = (
        P("row", "col"),
        P("row", "col"),
        P("col", None),
        P(("row", "col"), None),
        P(("row", "col"), None),
        P(("row", "col")),
        P(None, "col", None),
        P(None, "col", None),
    )
    return jax.shard_map(
        on_device, mesh=mesh, in_specs=placed, out_specs=P(("row", "col"), None), check_vma=False
    )
```

```python
import functools

import jax
import jax.numpy as jnp
from jax import lax
from jax.experimental import pallas as pl
from jax.experimental.pallas import tpu as pltpu
from jax.sharding import PartitionSpec as P

F32, BF16 = jnp.float32, jnp.bfloat16


def thin(x, mat, turned):
    n = x.shape[0]
    high = x.astype(BF16).astype(F32)
    both = jnp.concatenate([high, x - high], axis=0).astype(BF16)
    dims = (((1,), (1 if turned else 0,)), ((), ()))
    r = lax.dot_general(both, mat, dims, preferred_element_type=F32)
    return r[:n] + r[n:]


def split(ref, x):
    high = x.astype(BF16)
    ref[0] = high
    ref[1] = (x - high.astype(F32)).astype(BF16)


def pair_dot(lhs, rhs, dims):
    total = None
    for a in lhs:
        for b in rhs:
            r = lax.dot_general(a, b, (dims, ((), ())), preferred_element_type=F32)
            total = r if total is None else total + r
    return total


def counts(cols, levels):
    chips = cols
    mats = 2 * levels + 1
    swaps = levels + levels * (levels - 1) // 2
    remote = (
        4 * (cols // 2) - 1
        + 2 * cols - 1
        + mats * (2 * (cols // 2 - 1) + 1)
        + 1 + chips - 1
        + swaps
        + 2 * cols - 1
    )
    return chips, mats, swaps, remote


def kernel(
    cols, levels,
    near, pattern, iterate, right, basis, weight, transfers, inverses,
    out,
    near_v, iter_v, right_v, vfull, dfull, mats, part, corebuf, red, halfbuf,
    swap_out, swap_in, fin_out, fin_in, weighted, block, products, local_sem, send_sem, recv_sem,
):
    chips, n_mats, _, _ = counts(cols, levels)
    row, col = lax.axis_index("row"), lax.axis_index("col")
    leaf, half = row // 2, row % 2
    lane, core = col // 2, col % 2
    lanes = cols // 2
    chip = half * lanes + lane
    group = 2 * cols
    rhs = iterate.shape[1]
    n = rhs // group
    own_rows = basis.shape[0]
    mat_rows = transfers.shape[1]
    partner = (row, col + 1 - 2 * core)

    def chip_device(c, k):
        return (leaf * 2 + c // lanes, (c % lanes) * 2 + k)

    def place(c, k):
        return (c // lanes) * cols + (c % lanes) * 2 + k

    def rows_at(c, k, size):
        return pl.ds(pl.multiple_of(place(c, k) * size, size), size)

    def sibling(bit):
        b = (leaf // 2**bit) % 2
        return ((leaf + (1 - 2 * b) * 2**bit) * 2 + half, col)

    used = [0]
    started = []

    def send(src, dst, device):
        k = used[0]
        used[0] += 1
        copy = pltpu.make_async_remote_copy(
            src_ref=src, dst_ref=dst, send_sem=send_sem.at[k], recv_sem=recv_sem.at[k],
            device_id=device, device_id_type=pl.DeviceIdType.MESH,
        )
        copy.start()
        started.append(copy)
        return copy

    locals_used = [0]

    def local(src, dst):
        k = locals_used[0]
        locals_used[0] += 1
        copy = pltpu.make_async_copy(src, dst, local_sem.at[k])
        copy.start()
        return copy

    offsets = [(1, d) for d in range(1, lanes)] + [(1, 0)] + [(0, d) for d in range(1, lanes)]

    def ahead(o):
        return ((half + o[0]) % 2) * lanes + (lane + o[1]) % lanes

    def behind(o):
        return ((half + o[0]) % 2) * lanes + (lane + lanes - o[1]) % lanes

    barrier = pltpu.get_barrier_semaphore()
    others = []
    for d in range(chips):
        c = (chip + d) % chips
        if d > 0:
            others.append(chip_device(c, core))
        others.append(chip_device(c, 1 - core))
    others += [sibling(b) for b in range(levels)]
    for device in others:
        pl.semaphore_signal(
            barrier, inc=1, device_id=device, device_id_type=pl.DeviceIdType.MESH
        )
    mine = rows_at(chip, core, own_rows)
    near_copy = local(near, near_v)
    iter_copy = local(iterate, iter_v)
    mine_in_half = pl.ds(pl.multiple_of(col * own_rows, own_rows), own_rows)
    aligned = own_rows % 128 == 0
    if not aligned:
        right_v[...] = jnp.zeros_like(right_v)
    right_copy = local(right, right_v if aligned else right_v.at[mine_in_half])
    base_copy = local(basis, vfull.at[mine])
    weight_copy = local(weight, dfull.at[place(chip, core)])

    def source(m):
        k = m if m < levels else m - levels
        index = 2 * cols - (2 * cols // 2**k) + leaf // 2**k
        return (transfers if m < levels else inverses).at[index]

    order = list(range(levels)) + [levels + k for k in range(levels, -1, -1)]
    own_mat = pl.ds(pl.multiple_of(col * mat_rows, mat_rows), mat_rows)
    mat_local = {m: local(source(m), mats.at[m, own_mat]) for m in order}

    pl.semaphore_wait(barrier, len(others))

    across = ((leaf * 2 + 1 - half), col)
    base_lane = [
        send(basis, vfull.at[mine], (row, ((lane + d) % lanes) * 2 + core))
        for d in range(1, lanes)
    ]
    base_across = send(basis, vfull.at[mine], across)
    base_partner = send(basis, vfull.at[mine], partner)

    def base_slot(h, d):
        return vfull.at[rows_at(h * lanes + (lane + lanes - d) % lanes, core, own_rows)]

    weight_sends = []
    for d in range(chips):
        c = (chip + d) % chips
        for k in ([core, 1 - core] if d > 0 else [1 - core]):
            weight_sends.append(
                send(weight, dfull.at[place(chip, core)], chip_device(c, k))
            )
    mat_far, mat_near, mat_forward = {}, {}, {}

    def start_mat(m):
        mat_far[m] = [
            send(source(m), mats.at[m, own_mat], (row, ((lane + d) % lanes) * 2 + core))
            for d in range(1, lanes)
        ]
        mat_near[m] = send(source(m), mats.at[m, own_mat], partner)

    def forward_mat(m):
        mat_forward[m] = []
        for d in range(1, lanes):
            mat_far[m][d - 1].wait_recv()
            came = ((lane + lanes - d) % lanes) * 2 + core
            slot = mats.at[m, pl.ds(pl.multiple_of(came * mat_rows, mat_rows), mat_rows)]
            mat_forward[m].append(send(slot, slot, partner))

    def finish_mat(m):
        mat_local[m].wait()
        mat_near[m].wait_recv()
        for copy in mat_forward[m]:
            copy.wait_recv()

    start_mat(order[0])

    near_copy.wait()
    iter_copy.wait()
    right_copy.wait()
    present = pattern[0, 0].astype(F32)
    turned = lax.dot_general(
        iter_v[...], near_v[...], (((0,), (1,)), ((), ())), preferred_element_type=F32
    )
    if aligned:
        part[...] = -present * turned
        part[:, mine_in_half] = part[:, mine_in_half] + right_v[...].T
    else:
        part[...] = right_v[...].T - present * turned

    wide = rhs // 2
    core_send = send(
        part.at[pl.ds(pl.multiple_of((1 - core) * wide, wide), wide)], corebuf, partner
    )
    core_send.wait_recv()
    base_forward = []
    for d in range(1, lanes):
        base_lane[d - 1].wait_recv()
        base_forward.append(send(base_slot(half, d), base_slot(half, d), partner))
    applied = part[pl.ds(pl.multiple_of(core * wide, wide), wide), :] + corebuf[...]
    base_copy.wait()
    base_partner.wait_recv()
    for copy in base_forward:
        copy.wait_recv()
    half_rows = near.shape[0]
    half_base = vfull[pl.ds(pl.multiple_of(half * half_rows, half_rows), half_rows), :]
    red[...] = thin(applied, half_base, False)
    half_sends = []
    for o in offsets:
        c = ahead(o)
        half_sends.append(
            send(
                red.at[pl.ds(pl.multiple_of(c * n, n), n)],
                halfbuf.at[chip],
                chip_device(c, core),
            )
        )
    relays = [send(base_slot(half, d), base_slot(half, d), across) for d in range(1, lanes)]
    for m in order[1:]:
        start_mat(m)
    base_across.wait_recv()
    far_forward = [send(base_slot(1 - half, 0), base_slot(1 - half, 0), partner)]

    def forward_relays():
        for d in range(1, lanes):
            relays[d - 1].wait_recv()
            far_forward.append(send(base_slot(1 - half, d), base_slot(1 - half, d), partner))

    forward_mat(order[0])
    gathered = red[pl.ds(pl.multiple_of(chip * n, n), n), :]
    for o, copy in zip(offsets, half_sends):
        copy.wait_recv()
        gathered = gathered + halfbuf[behind(o)]
    swaps_used = [0]

    def swap_sum(x, bit, meanwhile=(), then=None):
        k = swaps_used[0]
        swaps_used[0] += 1
        swap_out[k] = x
        copy = send(swap_out.at[k], swap_in.at[k], sibling(bit))
        for m in meanwhile:
            forward_mat(m)
        if then is not None:
            then()
        copy.wait_recv()
        return x + swap_in[k]

    def form_leaf():
        weight_copy.wait()
        for copy in far_forward:
            copy.wait_recv()
        for copy in weight_sends:
            copy.wait_recv()
        weights = jnp.concatenate([dfull[p] for p in range(group)], axis=0).T
        for p in range(group):
            rows = pl.ds(p * own_rows, own_rows)
            scaled = weights[:, p:p + 1] * vfull[rows, :].astype(F32)
            high = scaled.astype(BF16)
            weighted[0, rows, :] = high
            weighted[1, rows, :] = (scaled - high.astype(F32)).astype(BF16)
        split(block, pair_dot([vfull[...]], [weighted[0], weighted[1]], ((0,), (0,))))

    def form_products():
        split(products.at[0], pair_dot([block[0], block[1]], [mats[0]], ((1,), (0,))))

    projected = [gathered]
    pending = order[1:]
    for k in range(levels):
        finish_mat(k)
        lifted = thin(projected[k], mats[k], False)
        now, pending = pending[:1], pending[1:]
        if k < levels - 1:
            projected.append(swap_sum(lifted, k, now, forward_relays if k == 0 else None))
        else:
            projected.append(swap_sum(lifted, k, now, form_leaf))
    finish_mat(2 * levels)
    correction = thin(projected[levels], mats[2 * levels], True)
    for k in range(levels - 1, -1, -1):
        if k == 0:
            s = thin(correction, products[0, 0], True) + thin(correction, products[0, 1], True)
        else:
            y = correction
            for j in range(k, -1, -1):
                y = thin(y, mats[j], True)
            s = thin(y, block[0], True) + thin(y, block[1], True)
        for j in range(k):
            s = thin(s, mats[j], False)
            s = swap_sum(s, j, pending[:1], form_products if k == 1 else None)
            pending = pending[1:]
        for m in pending[:1] if levels + k in pending else ():
            forward_mat(m)
            pending = pending[1:]
        finish_mat(levels + k)
        correction = thin(projected[k] - s, mats[levels + k], True)
    first = (core * chips + chip) * n
    slot = pl.ds(pl.multiple_of(first, n), n)
    fin_sends = []
    for step in (1, 0):
        side = (half + step) % 2
        base = vfull[pl.ds(pl.multiple_of(side * half_rows, half_rows), half_rows), :]
        rows = thin(correction, base, True)
        for p in range(cols):
            fin_out[side * cols + p] = rows[:, p * own_rows:(p + 1) * own_rows]
        for o in [o for o in offsets if o[0] == step] + ([(0, 0)] if step == 0 else []):
            c = ahead(o)
            for k in ([core, 1 - core] if o != (0, 0) else [1 - core]):
                fin_sends.append(
                    send(fin_out.at[place(c, k)], fin_in.at[slot], chip_device(c, k))
                )
    fin_in[slot, :] = fin_out[place(chip, core)]
    for copy in fin_sends:
        copy.wait_recv()
    out[...] = fin_in[...]
    for copy in started:
        copy.wait_send()


def on_device(near_blocks, pattern, iterate, right_side, basis, leaf_weight, transfers, inverses):
    cols = lax.axis_size("col")
    levels = cols.bit_length() - 1
    chips, n_mats, swaps, remote = counts(cols, levels)
    group = 2 * cols
    rank = basis.shape[1]
    own_rows = basis.shape[0]
    rhs = iterate.shape[1]
    n = rhs // group
    half_rows = near_blocks.shape[0]
    any_spec = pl.BlockSpec(memory_space=pl.ANY)
    turned = pl.pallas_call(
        functools.partial(kernel, cols, levels),
        out_shape=pltpu.VMEM((rhs, own_rows), F32),
        in_specs=[any_spec, pl.BlockSpec(memory_space=pltpu.SMEM)] + [any_spec] * 6,
        out_specs=pl.BlockSpec(memory_space=pltpu.VMEM),
        scratch_shapes=[
            pltpu.VMEM(near_blocks.shape, BF16),
            pltpu.VMEM(iterate.shape, BF16),
            pltpu.VMEM((own_rows if own_rows % 128 == 0 else half_rows, rhs), F32),
            pltpu.VMEM((2 * half_rows, rank), BF16),
            pltpu.VMEM((group, 1, own_rows), F32),
            pltpu.VMEM((n_mats, rank, rank), BF16),
            pltpu.VMEM((rhs, half_rows), F32),
            pltpu.VMEM((rhs // 2, half_rows), F32),
            pltpu.VMEM((rhs // 2, rank), F32),
            pltpu.VMEM((chips, n, rank), F32),
            pltpu.VMEM((swaps, n, rank), F32),
            pltpu.VMEM((swaps, n, rank), F32),
            pltpu.VMEM((group, n, own_rows), F32),
            pltpu.VMEM((rhs, own_rows), F32),
            pltpu.VMEM((2, 2 * half_rows, rank), BF16),
            pltpu.VMEM((2, rank, rank), BF16),
            pltpu.VMEM((levels, 2, rank, rank), BF16),
            pltpu.SemaphoreType.DMA((5 + n_mats,)),
            pltpu.SemaphoreType.DMA((remote,)),
            pltpu.SemaphoreType.DMA((remote,)),
        ],
        compiler_params=pltpu.CompilerParams(collective_id=0, has_side_effects=True),
    )(
        near_blocks, pattern, iterate, right_side, basis,
        leaf_weight.reshape(1, own_rows), transfers, inverses,
    )
    return turned.T


def solution(mesh):
    placed = (
        P("row", "col"),
        P("row", "col"),
        P("col", None),
        P(("row", "col"), None),
        P(("row", "col"), None),
        P(("row", "col")),
        P(None, "col", None),
        P(None, "col", None),
    )
    return jax.shard_map(
        on_device, mesh=mesh, in_specs=placed, out_specs=P(("row", "col"), None), check_vma=False
    )
```
